32 devices in a mesh: grp: 8 (over z, x), dev: 4 (over y, core).
Axes of the slice: x: 2, y: 2, z: 4, core: 2. Of those that a mesh axis runs over, the one named last changes fastest.
Arguments:
- block_states: float32 [256, 5, 4096], P(('grp', 'dev')), may hold values from -2 to 10.5, as said below
- dest_dev: int32 [256], P('grp'), may hold values from -1 to 3, as said below
- dest_slot: int32 [256], P('grp'), may hold values from 0 to 3, as said below
- neighbours: int32 [2, 128], P(None, 'grp'), may hold values from -1 to 15, as said below
- coarse_map: int32 [4, 32], P('dev'), may hold values from 0 to 31, each once within a row
Outputs:
- advanced: float32 [128, 5, 4096], P(('grp', 'dev'))
- registers: float32 [32, 5, 256], P(('grp', 'dev'))
The draws below stay inside these ranges and needn't reach their ends.
Inputs may be any that keep to these rules, and one draw needn't show every extreme that they name: `block_states`: every slot holds a physical state: density 0.5 to 2, each velocity component -1 to 1, pressure 0.3 to 3. `dest_dev`: each pair of a receiving device index and a slot 0 .. 3 of a group gets exactly one patch; a device keeps its own patches or sends at most one patch to each of the next 3 device indices of its group (counted modulo 4) and to no other. `dest_slot`: see dest_dev. Index dev * 4 + slot within the group; neighbours are mutual (neighbours[1, a] = b exactly when neighbours[0, b] = a, within a group), a neighbour's index differs from the patch's own by at most 3, and -1 marks a domain boundary. `coarse_map`: for each device index a permutation: value m names register m // 4 in the group order, quadrant m % 4.
All inputs are finite; a program needn't handle non-finite values.
Results may differ from the reference program's by a relative error of at most 0.0003.
Values sent between devices are 32-bit elements; how exact they have to be, the bound alone decides.
No kernel may reach another device: no remote copies, remote signals or barrier semaphores. Data moves between devices by JAX's collectives and lax.ppermute only.
A program may use at most 64 MiB of HBM per device.

```python
import math
import jax
import jax.numpy as jnp
from jax import lax

SIDE_LENGTH = 16
STATE_VARIABLES = 5
DEVICE_PATCHES = 4
P_DEV = 8
SLOTS_IN = 256
BLOCK_NUMBER = 128
REGS = 32
N_GRP = 8
N_DEV = 4


def rebalance_plan(key):
    base_key = jax.random.fold_in(key, 11)
    key_bits = jax.random.fold_in(base_key, 1)
    key_slots = jax.random.fold_in(base_key, 2)
    offsets = jnp.broadcast_to(jnp.arange(1, DEVICE_PATCHES, dtype=jnp.int32), (N_GRP, DEVICE_PATCHES - 1))
    bits = jax.random.randint(key_bits, (N_GRP, N_DEV, DEVICE_PATCHES - 1), 0, 2)
    sources = jnp.arange(N_DEV, dtype=jnp.int32)[None, :, None]
    receivers = ((sources + offsets[:, None, :]) % N_DEV).astype(jnp.int32)
    sending = jnp.take_along_axis(bits, receivers, axis=1)
    staying = jnp.concatenate([jnp.ones((N_GRP, N_DEV, 1), jnp.int32), 1 - bits], axis=2)
    stay_dev = jnp.where(staying == 1, jnp.broadcast_to(sources, staying.shape), -1)
    send_dev = jnp.where(sending == 1, receivers, -1)
    cand_dev = jnp.concatenate([stay_dev, send_dev, -jnp.ones((N_GRP, N_DEV, 1), jnp.int32)], axis=2).astype(jnp.int32)
    stay_slot = jnp.broadcast_to(jnp.arange(DEVICE_PATCHES, dtype=jnp.int32), (N_GRP, N_DEV, DEVICE_PATCHES))
    send_slot = jnp.broadcast_to(jnp.arange(1, DEVICE_PATCHES, dtype=jnp.int32), (N_GRP, N_DEV, DEVICE_PATCHES - 1))
    cand_slot = jnp.concatenate([stay_slot, send_slot, jnp.zeros((N_GRP, N_DEV, 1), jnp.int32)], axis=2)
    cand_slot = jnp.where(cand_dev >= 0, cand_slot, 0)
    order = jax.vmap(lambda subkey: jax.random.permutation(subkey, 2 * DEVICE_PATCHES))(jax.random.split(key_slots, N_GRP * N_DEV))
    order = order.reshape(N_GRP, N_DEV, 2 * DEVICE_PATCHES).astype(jnp.int32)
    dest_dev = jnp.take_along_axis(cand_dev, order, axis=2).reshape(-1).astype(jnp.int32)
    dest_slot = jnp.take_along_axis(cand_slot, order, axis=2).reshape(-1).astype(jnp.int32)
    return (dest_dev, dest_slot)


def draw_dest_dev(key, part):
    return rebalance_plan(key)[0]


def draw_dest_slot(key, part):
    return rebalance_plan(key)[1]


def draw_neighbours(key, part):
    key_swap, key_cut = jax.random.split(jax.random.fold_in(key, 37))
    group_size = N_DEV * DEVICE_PATCHES
    position = jnp.arange(group_size, dtype=jnp.int32)
    swapping = jax.random.randint(key_swap, (N_GRP, group_size // 2, 1), 0, 2)
    paired = position.reshape(1, group_size // 2, 2)
    flipped = paired[:, :, ::-1]
    order = jnp.where(swapping == 1, flipped, paired).reshape(N_GRP, group_size).astype(jnp.int32)
    cutting = jax.random.randint(key_cut, (N_GRP, group_size - 1), 0, 8) == 0
    cutting = cutting & (jnp.arange(group_size - 1, dtype=jnp.int32)[None, :] < group_size - 4)
    lower_pos = jnp.concatenate([-jnp.ones((N_GRP, 1), jnp.int32), jnp.where(cutting, -1, order[:, :-1])], axis=1)
    upper_pos = jnp.concatenate([jnp.where(cutting, -1, order[:, 1:]), -jnp.ones((N_GRP, 1), jnp.int32)], axis=1)
    lower = jnp.take_along_axis(lower_pos, order, axis=1).reshape(-1)
    upper = jnp.take_along_axis(upper_pos, order, axis=1).reshape(-1)
    return jnp.stack([lower, upper], axis=0).astype(jnp.int32)


def draw_block_states(key, part):
    keys = jax.random.split(jax.random.fold_in(key, 23), 7)
    shape = (SLOTS_IN, SIDE_LENGTH ** 3)
    density = jax.random.uniform(keys[0], shape, jnp.float32, 0.5, 2.0)
    vel_x = jax.random.uniform(keys[1], shape, jnp.float32, -1.0, 1.0)
    vel_y = jax.random.uniform(keys[2], shape, jnp.float32, -1.0, 1.0)
    vel_z = jax.random.uniform(keys[6], shape, jnp.float32, -1.0, 1.0)
    pressure = jnp.exp(jax.random.uniform(keys[3], shape, jnp.float32, math.log(0.3), math.log(3.0)))
    energy = pressure / 0.4 + 0.5 * density * (vel_x * vel_x + vel_y * vel_y + vel_z * vel_z)
    stacked = jnp.stack([density, density * vel_x, density * vel_y, density * vel_z, energy], axis=1)
    return stacked.astype(jnp.float32)


def setup_inputs(seed: int = 0) -> dict:
    seeds = jax.random.split(jax.random.key(seed), 6)
    return {
        "block_states": draw_block_states(jax.random.fold_in(seeds[5], 71), 0),
        "dest_dev": draw_dest_dev(jax.random.fold_in(seeds[5], 71), 0),
        "dest_slot": draw_dest_slot(jax.random.fold_in(seeds[5], 71), 0),
        "neighbours": draw_neighbours(jax.random.fold_in(seeds[5], 71), 0),
        "coarse_map": jax.vmap(lambda own: jax.random.permutation(own, N_GRP * DEVICE_PATCHES))(jax.random.split(seeds[4], N_DEV)).reshape((N_DEV, N_GRP * DEVICE_PATCHES)).astype(jnp.int32),
    }


GAMMA = 1.4
COURANT = 0.2

def primitives(conserved):
    density = conserved[..., 0, :, :]
    inverse = 1.0 / density
    vel_x = conserved[..., 1, :, :] * inverse
    vel_y = conserved[..., 2, :, :] * inverse
    vel_z = conserved[..., 3, :, :] * inverse
    kinetic = 0.5 * (conserved[..., 1, :, :] * vel_x + conserved[..., 2, :, :] * vel_y + conserved[..., 3, :, :] * vel_z)
    pressure = (GAMMA - 1.0) * (conserved[..., 4, :, :] - kinetic)
    return jnp.stack([density, vel_x, vel_y, vel_z, pressure], axis=-3)

def euler_flux(primitive):
    density = primitive[..., 0, :, :]
    vel_x = primitive[..., 1, :, :]
    vel_y = primitive[..., 2, :, :]
    vel_z = primitive[..., 3, :, :]
    pressure = primitive[..., 4, :, :]
    mass_flux = density * vel_x
    energy = pressure / (GAMMA - 1.0) + 0.5 * density * (vel_x * vel_x + vel_y * vel_y + vel_z * vel_z)
    fluxes = jnp.stack([mass_flux, mass_flux * vel_x + pressure, mass_flux * vel_y, mass_flux * vel_z, vel_x * (energy + pressure)], axis=-3)
    conserved = jnp.stack([density, mass_flux, density * vel_y, density * vel_z, energy], axis=-3)
    speeds = jnp.abs(vel_x) + jnp.sqrt(GAMMA * pressure / density)
    return (fluxes, conserved, speeds)

def advance(block_volumes, lower_ghost, upper_ghost):
    extended = jnp.concatenate([lower_ghost, block_volumes, upper_ghost], axis=-2)
    primitive = primitives(extended)
    below_diff = primitive[..., 1:-1, :] - primitive[..., :-2, :]
    above_diff = primitive[..., 2:, :] - primitive[..., 1:-1, :]
    slopes = 0.5 * (jnp.sign(below_diff) + jnp.sign(above_diff)) * jnp.minimum(jnp.abs(below_diff), jnp.abs(above_diff))
    centre = primitive[..., 1:-1, :]
    left_state = (centre + 0.5 * slopes)[..., :-1, :]
    right_state = (centre - 0.5 * slopes)[..., 1:, :]
    left_flux, left_cons, left_speed = euler_flux(left_state)
    right_flux, right_cons, right_speed = euler_flux(right_state)
    largest = jnp.maximum(left_speed, right_speed)[..., None, :, :]
    interface = 0.5 * (left_flux + right_flux) - 0.5 * largest * (right_cons - left_cons)
    updated = block_volumes - COURANT * (interface[..., 1:, :] - interface[..., :-1, :])
    return (updated, interface[..., -1, :])

def fill_edges(block_volumes, lower_ghost, upper_ghost, lower_nbr, upper_nbr):
    first = block_volumes[:, :, :1, :]
    last = block_volumes[:, :, -1:, :]
    lower_ghost = jnp.where((lower_nbr < 0)[:, None, None, None], jnp.concatenate([first, first], axis=2), lower_ghost)
    upper_ghost = jnp.where((upper_nbr < 0)[:, None, None, None], jnp.concatenate([last, last], axis=2), upper_ghost)
    return (lower_ghost, upper_ghost)

def coarsen(interface):
    half_edge = SIDE_LENGTH // 2
    shaped = interface.reshape(interface.shape[:-1] + (half_edge, 2, half_edge, 2))
    return shaped.mean(axis=(-3, -1))

def spread(coarse, quadrant):
    half_edge = SIDE_LENGTH // 2
    tiled = jnp.tile(coarse, (1,) * (coarse.ndim - 2) + (2, 2))
    row_ids = jnp.arange(SIDE_LENGTH, dtype=jnp.int32) // half_edge
    inside = (row_ids[:, None] == (quadrant // 2)[..., None, None]) & (row_ids[None, :] == (quadrant % 2)[..., None, None])
    placed = tiled * inside.astype(tiled.dtype)[..., None, :, :]
    return placed.reshape(placed.shape[:-2] + (SIDE_LENGTH * SIDE_LENGTH,))

def reference(block_states, dest_dev, dest_slot, neighbours, coarse_map):
    group_size = N_DEV * DEVICE_PATCHES
    slot_group = jnp.arange(SLOTS_IN, dtype=jnp.int32) // (N_DEV * P_DEV)
    destination_position = jnp.where(dest_dev >= 0, (slot_group * N_DEV + dest_dev) * DEVICE_PATCHES + dest_slot, BLOCK_NUMBER).astype(jnp.int32)
    redistributed_blocks = jnp.zeros((BLOCK_NUMBER, STATE_VARIABLES, SIDE_LENGTH ** 3), block_states.dtype).at[destination_position].set(block_states, mode='drop')
    block_volumes = redistributed_blocks.reshape(BLOCK_NUMBER, STATE_VARIABLES, SIDE_LENGTH, SIDE_LENGTH * SIDE_LENGTH)
    slot_index = jnp.arange(BLOCK_NUMBER, dtype=jnp.int32)
    group_start = slot_index // group_size * group_size
    lower_src = jnp.where(neighbours[0] >= 0, group_start + neighbours[0], slot_index).astype(jnp.int32)
    upper_src = jnp.where(neighbours[1] >= 0, group_start + neighbours[1], slot_index).astype(jnp.int32)
    lower_ghost = block_volumes[:, :, SIDE_LENGTH - 2:, :][lower_src]
    upper_ghost = block_volumes[:, :, :2, :][upper_src]
    lower_ghost, upper_ghost = fill_edges(block_volumes, lower_ghost, upper_ghost, neighbours[0], neighbours[1])

    def one_group(operands):
        return advance(operands[0], operands[1], operands[2])
    advanced, interface = lax.map(one_group, (block_volumes.reshape(N_GRP, group_size, STATE_VARIABLES, SIDE_LENGTH, SIDE_LENGTH * SIDE_LENGTH), lower_ghost.reshape(N_GRP, group_size, STATE_VARIABLES, 2, SIDE_LENGTH * SIDE_LENGTH), upper_ghost.reshape(N_GRP, group_size, STATE_VARIABLES, 2, SIDE_LENGTH * SIDE_LENGTH)))
    advanced = advanced.reshape(BLOCK_NUMBER, STATE_VARIABLES, SIDE_LENGTH ** 3)
    interface = interface.reshape(BLOCK_NUMBER, STATE_VARIABLES, SIDE_LENGTH * SIDE_LENGTH)
    values = coarse_map.reshape(N_DEV, N_GRP, DEVICE_PATCHES).transpose(1, 0, 2).reshape(BLOCK_NUMBER)
    device = slot_index // DEVICE_PATCHES % N_DEV
    owner = (values // DEVICE_PATCHES * N_DEV + device).astype(jnp.int32)
    placed = spread(coarsen(interface), values % DEVICE_PATCHES)
    registers = jax.ops.segment_sum(placed, owner, num_segments=REGS)
    return (advanced, registers)
```

```python
import functools

import jax
import jax.numpy as jnp
from jax import lax
from jax.experimental import pallas as pl
from jax.experimental.pallas import tpu as pltpu
from jax.sharding import PartitionSpec as P

SIDE = 16
FIELDS = 5
KEEP = 4
REACH = 4
LANES = 128
HALVES = SIDE * SIDE // LANES
TILES = SIDE * HALVES
GROUP = HALVES * KEEP
GHOST = FIELDS * 2 * GROUP
TOPS = FIELDS * 2 * HALVES
PATCH = FIELDS * TILES
COARSE = 16

GAMMA = 1.4
COURANT = 0.2

VMEM = pl.BlockSpec(memory_space=pltpu.VMEM)
SMEM = pl.BlockSpec(memory_space=pltpu.SMEM)
HBM = pl.BlockSpec(memory_space=pltpu.HBM)


def rows(count):
    return jax.ShapeDtypeStruct((count, LANES), jnp.float32)


def params():
    return pltpu.CompilerParams(vmem_limit_bytes=8 * 1024 * 1024)


def primitives(u):
    inverse = 1.0 / u[0]
    vx, vy, vz = u[1] * inverse, u[2] * inverse, u[3] * inverse
    kinetic = 0.5 * (u[1] * vx + u[2] * vy + u[3] * vz)
    return [u[0], vx, vy, vz, (GAMMA - 1.0) * (u[4] - kinetic)]


def half_slopes(below, above):
    return [
        0.5 * (jnp.maximum(jnp.minimum(a, b), 0.0) + jnp.minimum(jnp.maximum(a, b), 0.0))
        for a, b in zip(below, above)
    ]


def euler_flux(state):
    r, vx, vy, vz, p = state
    mass = r * vx
    energy = p * (1.0 / (GAMMA - 1.0)) + 0.5 * r * (vx * vx + vy * vy + vz * vz)
    flux = [mass, mass * vx + p, mass * vy, mass * vz, vx * (energy + p)]
    conserved = [r, mass, r * vy, r * vz, energy]
    return flux, conserved, jnp.abs(vx) + jnp.sqrt(GAMMA * p / r)


def interface_flux(left, right):
    lf, lc, ls = euler_flux(left)
    rf, rc, rs = euler_flux(right)
    half = 0.5 * jnp.maximum(ls, rs)
    return [0.5 * (a + b) - half * (d - c) for a, b, c, d in zip(lf, rf, lc, rc)]


def pack_kernel(n, slots, deltas, dev_hbm, slot_hbm, nbr_hbm, x_hbm, *refs):
    count = len(deltas)
    early = refs[:count]
    late = refs[count : 2 * count]
    own, x, plan, dev, slot, nbr, inv, sems = refs[2 * count :]
    copies = [
        pltpu.make_async_copy(src, dst, sems.at[i])
        for i, (src, dst) in enumerate(
            ((x_hbm, x), (dev_hbm, dev), (slot_hbm, slot), (nbr_hbm, nbr))
        )
    ]
    for copy in copies:
        copy.start()
    me = lax.axis_index("dev")
    total = n * slots
    for copy in copies[1:]:
        copy.wait()

    def invert(i, carry):
        to = dev[i]
        inv[jnp.where(to >= 0, to * KEEP + slot[i], n * KEEP)] = i
        return carry

    if total <= 64:
        for i in range(total):
            invert(i, 0)
    else:
        lax.fori_loop(0, total, invert, 0)

    def held(p):
        i = inv[p]
        holder = lax.div(i, slots)
        return holder == me, lax.rem(i, slots), holder

    def ghost(side, p, mine, at):
        near = nbr[side, p]
        edge = near < 0
        nbr_mine, nbr_at, _ = held(jnp.maximum(near, 0))
        valid = jnp.where(edge, mine, nbr_mine).astype(jnp.float32)
        first, second = (TILES - 2 * HALVES, TILES - HALVES) if side == 0 else (0, HALVES)
        flat = 0 if side == 0 else TILES - HALVES
        source = jnp.where(edge, at, nbr_at)
        return (
            valid,
            jnp.where(edge, flat, first) * slots + source,
            jnp.where(edge, flat, second) * slots + source,
        )

    wanted = []
    for delta in (0,) + deltas:
        c = me + delta
        c = jnp.where(c >= n, c - n, c)
        label, patch_at = jnp.float32(-1.0), jnp.int32(0)
        faces = []
        for q in range(KEEP):
            p = c * KEEP + q
            mine, at, holder = held(p)
            label = jnp.where(mine, jnp.float32(q), label)
            patch_at = jnp.where(mine, at, patch_at)
            faces.append((mine, at, ghost(0, p, mine, at), ghost(1, p, mine, at)))
            if delta == 0:
                away = me - holder
                plan[q] = jnp.where(away < 0, away + n, away)
                plan[KEEP + q] = at
        wanted.append((label, patch_at, faces))
    copies[0].wait()

    def put_ghost(ref, base, q, where):
        valid, first, second = where
        for f in range(FIELDS):
            at = f * TILES * slots
            for layer, start in enumerate((first, second)):
                v = x[pl.ds(at + start, HALVES, stride=slots), :] * valid
                ref[pl.ds(base + (f * 2 + layer) * GROUP + q, HALVES, stride=KEEP), :] = v

    top = (TILES - 2 * HALVES) * slots
    for k, delta in enumerate(deltas):
        label, patch_at, faces = wanted[1 + k]
        for q in range(KEEP):
            put_ghost(early[k], 0, q, faces[q][3])
        if delta < REACH:
            for f in range(FIELDS):
                early[k][pl.ds(GHOST + f * 2 * HALVES, 2 * HALVES), :] = x[
                    pl.ds(f * TILES * slots + top + patch_at, 2 * HALVES, stride=slots), :
                ]
            early[k][pl.ds(GHOST + TOPS, 4), :] = jnp.full((4, LANES), label, jnp.float32)
    for k, delta in enumerate(deltas):
        _, patch_at, faces = wanted[1 + k]
        base = 0
        if delta < REACH:
            base = PATCH
            for t in range(0, PATCH, 8):
                late[k][pl.ds(t, 8), :] = x[pl.ds(t * slots + patch_at, 8, stride=slots), :]
        for q in range(KEEP):
            put_ghost(late[k], base, q, faces[q][2])
    for q, (mine, at, lower, upper) in enumerate(wanted[0][2]):
        kept = mine.astype(jnp.float32)
        put_ghost(own, 0, q, (kept, top + at, top + HALVES * slots + at))
        put_ghost(own, GHOST, q, upper)
        put_ghost(own, 2 * GHOST, q, lower)


def layer(ref, base, f, number):
    return ref[pl.ds(base + (f * 2 + number) * GROUP, GROUP), :]


def coarse_kernel(deltas, *refs):
    early = refs[: len(deltas)]
    own, out = refs[len(deltas) :]
    row = lax.broadcasted_iota(jnp.int32, (GROUP, LANES), 0)
    lane = lax.broadcasted_iota(jnp.int32, (GROUP, LANES), 1)
    which = lax.rem(row, KEEP)
    half = lax.div(row, KEEP)
    place = which.astype(jnp.float32)
    patches = [
        (e, jnp.broadcast_to(e[pl.ds(GHOST + TOPS, 1), :], (GROUP, LANES)) == place)
        for e, delta in zip(early, deltas)
        if delta < REACH
    ]

    def top_layer(f, number):
        total = layer(own, 0, f, number)
        for e, mask in patches:
            at = GHOST + (f * 2 + number) * HALVES
            v = jnp.where(half == 0, e[pl.ds(at, 1), :], e[pl.ds(at + 1, 1), :])
            total = total + jnp.where(mask, v, 0.0)
        return total

    def upper_layer(f, number):
        total = layer(own, GHOST, f, number)
        for e in early:
            total = total + layer(e, 0, f, number)
        return total

    a0, a1 = (primitives([top_layer(f, i) for f in range(FIELDS)]) for i in range(2))
    b0, b1 = (primitives([upper_layer(f, i) for f in range(FIELDS)]) for i in range(2))
    d0 = [b - a for a, b in zip(a0, a1)]
    d1 = [b - a for a, b in zip(a1, b0)]
    d2 = [b - a for a, b in zip(b0, b1)]
    left = [a + s for a, s in zip(a1, half_slopes(d0, d1))]
    right = [b - s for b, s in zip(b0, half_slopes(d1, d2))]
    flux = jnp.concatenate(interface_flux(left, right), axis=0)
    fine = lax.broadcasted_iota(jnp.int32, (LANES, LANES), 0)
    spot = lax.broadcasted_iota(jnp.int32, (LANES, LANES), 1)
    edge = SIDE // 2
    same_y = lax.div(fine, 2 * SIDE) == lax.rem(lax.div(spot, SIDE), edge // 2)
    same_z = lax.rem(lax.div(fine, 2), edge) == lax.rem(spot, edge)
    mean = jnp.where(same_y & same_z, 0.25, 0.0)
    spread = jnp.dot(
        flux, mean, precision=lax.Precision.HIGHEST, preferred_element_type=jnp.float32
    )
    keep = (lax.div(lane, LANES // HALVES) == half) & (
        lax.rem(lax.div(lane, edge), 2) == lax.rem(which, 2)
    )
    out[...] = jnp.zeros_like(out)
    for f in range(FIELDS):
        v = jnp.where(keep, spread[f * GROUP : (f + 1) * GROUP], 0.0)
        v = v[:KEEP] + v[KEEP:]
        out[pl.ds(2 * f, 1), :] = v[0:1] + v[1:2]
        out[pl.ds(2 * f + 1, 1), :] = v[2:3] + v[3:4]


def step_kernel(n, slots, groups, butterfly, deltas, plan, cmap, x, own, *refs):
    count = len(deltas)
    early = refs[:count]
    late = refs[count : 2 * count]
    out, codes, ext = refs[2 * count :]
    span = (SIDE + 4) * GROUP
    lows = [PATCH if delta < REACH else 0 for delta in deltas]
    for f in range(FIELDS):
        for number in range(2):
            lower = layer(own, 2 * GHOST, f, number)
            upper = layer(own, GHOST, f, number)
            for e, v, low in zip(early, late, lows):
                lower = lower + layer(v, low, f, number)
                upper = upper + layer(e, 0, f, number)
            ext[pl.ds(f * span + number * GROUP, GROUP), :] = lower
            ext[pl.ds(f * span + (SIDE + 2 + number) * GROUP, GROUP), :] = upper
    for q in range(KEEP):
        source, at = plan[q], plan[KEEP + q]

        def fill(read, q=q):
            for f in range(FIELDS):
                for t in range(0, TILES, 8):
                    to = f * span + 2 * GROUP + t * KEEP + q
                    ext[pl.ds(to, 8, stride=KEEP), :] = read(f * TILES + t)

        @pl.when(source == 0)
        def _():
            fill(lambda t: x[pl.ds(t * slots + at, 8, stride=slots), :])

        for delta, ref in zip(deltas, late):
            if delta < REACH:

                @pl.when(source == delta)
                def _(ref=ref):
                    fill(lambda t: ref[pl.ds(t, 8), :])

    def cells(k):
        return [ext[pl.ds(f * span + k * GROUP, GROUP), :] for f in range(FIELDS)]

    p0, p1 = primitives(cells(0)), primitives(cells(1))
    mid = primitives(cells(2))
    below = [b - a for a, b in zip(p0, p1)]
    above = [b - a for a, b in zip(p1, mid)]
    left = [a + s for a, s in zip(p1, half_slopes(below, above))]
    before = None
    for j in range(SIDE + 1):
        ahead = primitives(cells(j + 3))
        diff = [b - a for a, b in zip(mid, ahead)]
        slopes = half_slopes(above, diff)
        right = [a - s for a, s in zip(mid, slopes)]
        flux = interface_flux(left, right)
        if before is not None:
            u = cells(j + 1)
            for f in range(FIELDS):
                v = u[f] - COURANT * (flux[f] - before[f])
                for h in range(HALVES):
                    out[f, (j - 1) * HALVES + h] = v[h * KEEP : (h + 1) * KEEP]
        left = [a + s for a, s in zip(mid, slopes)]
        before, mid, above = flux, ahead, diff

    me = lax.axis_index("grp")
    odd = lax.rem(lax.div(lax.broadcasted_iota(jnp.int32, (1, LANES), 1), SIDE // 2), 2) == 1
    for r in range(groups):
        g = lax.bitwise_xor(me, r) if butterfly else jnp.int32(r)
        quadrant = []
        for q in range(KEEP):
            m = cmap[0, g * KEEP + q]
            quadrant.append(jnp.where(lax.div(m, KEEP) == me, lax.rem(m, KEEP), -1))
        for pair in range(2):
            codes[pl.ds(pair * groups + r, 1), :] = jnp.where(
                odd, quadrant[2 * pair + 1], quadrant[2 * pair]
            )


def register_kernel(groups, faces, codes, out):
    edge = SIDE // 2
    lane = lax.broadcasted_iota(jnp.int32, (8, LANES), 1)
    odd = lax.rem(lax.div(lane, edge), 2)
    for f in range(FIELDS):
        sums = [jnp.zeros((8, LANES), jnp.float32) for _ in range(4)]
        for r in range(0, groups, 8):
            for pair in range(2):
                v = faces[pl.ds(r * COARSE + 2 * f + pair, 8, stride=COARSE), :]
                code = codes[pl.ds(pair * groups + r, 8), :]
                sums = [s + jnp.where(code == t, v, 0.0) for t, s in enumerate(sums)]
        for h in range(HALVES):
            even_q, odd_q = sums[2 * h], sums[2 * h + 1]
            even_q = even_q + pltpu.roll(even_q, LANES - edge, 1)
            odd_q = odd_q + pltpu.roll(odd_q, edge, 1)
            v = jnp.where(odd == 0, even_q, odd_q)
            out[f, :, pl.ds(h * LANES, LANES)] = jnp.sum(v, axis=0, keepdims=True)


def exchange(block, groups):
    stride = 1
    while stride < groups:
        route = [(i, i ^ stride) for i in range(groups)]
        block = jnp.concatenate([block, lax.ppermute(block, "grp", route)], axis=0)
        stride *= 2
    return block


def local(block_states, dest_dev, dest_slot, neighbours, coarse_map):
    n = lax.axis_size("dev")
    groups = lax.axis_size("grp")
    slots = block_states.shape[0]
    deltas = tuple(sorted({delta % n for delta in range(-1, REACH + 1)} - {0}))
    butterfly = groups & (groups - 1) == 0
    x = block_states.reshape(slots, FIELDS, TILES, LANES).transpose(1, 2, 0, 3)
    x = x.reshape(FIELDS * TILES * slots, LANES)
    early_rows = [GHOST + (TOPS + 4 if delta < REACH else 0) for delta in deltas]
    late_rows = [GHOST + (PATCH if delta < REACH else 0) for delta in deltas]
    count = len(deltas)
    *sent, own, x, plan = pl.pallas_call(
        functools.partial(pack_kernel, n, slots, deltas),
        out_shape=[rows(r) for r in early_rows + late_rows]
        + [rows(3 * GHOST), rows(x.shape[0]), jax.ShapeDtypeStruct((2 * KEEP,), jnp.int32)],
        in_specs=[HBM] * 4,
        out_specs=[VMEM] * (2 * count + 2) + [SMEM],
        scratch_shapes=[
            pltpu.SMEM(dest_dev.shape, jnp.int32),
            pltpu.SMEM(dest_slot.shape, jnp.int32),
            pltpu.SMEM(neighbours.shape, jnp.int32),
            pltpu.SMEM((n * KEEP + 1,), jnp.int32),
            pltpu.SemaphoreType.DMA((4,)),
        ],
        compiler_params=params(),
        name="pack",
    )(dest_dev, dest_slot, neighbours, x)
    routes = [[(i, (i + delta) % n) for i in range(n)] for delta in deltas]
    order = range(count - 1, -1, -1)
    early, late = [None] * count, [None] * count
    for k in order:
        early[k] = lax.ppermute(sent[k], "dev", routes[k])
    for k in order:
        late[k] = lax.ppermute(sent[count + k], "dev", routes[k])
    faces = pl.pallas_call(
        functools.partial(coarse_kernel, deltas),
        out_shape=rows(COARSE),
        in_specs=[VMEM] * (count + 1),
        out_specs=VMEM,
        compiler_params=params(),
        name="coarse",
    )(*early, own)
    if butterfly:
        faces = exchange(faces, groups)
    else:
        faces = lax.all_gather(faces, "grp", axis=0, tiled=True)
    advanced, codes = pl.pallas_call(
        functools.partial(step_kernel, n, slots, groups, butterfly, deltas),
        out_shape=[
            jax.ShapeDtypeStruct((FIELDS, TILES, KEEP, LANES), jnp.float32),
            jax.ShapeDtypeStruct((2 * groups, LANES), jnp.int32),
        ],
        in_specs=[SMEM, SMEM] + [VMEM] * (2 + 2 * count),
        out_specs=[VMEM, VMEM],
        scratch_shapes=[pltpu.VMEM((FIELDS * (SIDE + 4) * GROUP, LANES), jnp.float32)],
        compiler_params=params(),
        name="step",
    )(plan, coarse_map, x, own, *early, *late)
    registers = pl.pallas_call(
        functools.partial(register_kernel, groups),
        out_shape=jax.ShapeDtypeStruct((FIELDS, 1, SIDE * SIDE), jnp.float32),
        in_specs=[VMEM, VMEM],
        out_specs=VMEM,
        compiler_params=params(),
        name="registers",
    )(faces, codes)
    advanced = advanced.transpose(2, 0, 1, 3).reshape(KEEP, FIELDS, TILES * LANES)
    return (advanced, registers.transpose(1, 0, 2))


def solution(mesh):
    in_specs = (P(("grp", "dev"), None, None), P("grp"), P("grp"), P(None, "grp"), P("dev", None))
    out_specs = (P(("grp", "dev"), None, None), P(("grp", "dev"), None, None))
    return jax.shard_map(local, mesh=mesh, in_specs=in_specs, out_specs=out_specs, check_vma=False)
```
